32 devices in a mesh: row: 16 (over z, x, core), col: 2 (over y).
Axes of the slice: x: 2, y: 2, z: 4, core: 2. Of those that a mesh axis runs over, the one named last changes fastest.
Arguments:
- teacher_hidden: bfloat16 [512, 4608], P('row', 'col'), as said below
- student_hidden: bfloat16 [512, 3584], P('row', 'col'), as said below
- teacher_embed: bfloat16 [16384, 4608], P(('row', 'col')), may hold values from -0.4861359 to 0.4861359
- student_embed: bfloat16 [16384, 3584], P(('row', 'col')), may hold values from -0.5512263 to 0.5512263
Outputs:
- divergence: float32 [512], P(('row', 'col'))
- mean_divergence: float32 [], replicated
The draws below stay inside these ranges and needn't reach their ends.
Inputs may be any that keep to these rules, and one draw needn't show every extreme that they name: `teacher_hidden`: entries of order one; a few rows may be far larger. `student_hidden`: entries of order one; a few rows may be far larger.
All inputs are finite; a program needn't handle non-finite values.
Results may differ from the reference program's by a relative error of at most 0.0003.
Values may be sent and summed in bfloat16 or wider, within the bound.
A program may use at most 64 MiB of HBM per device.

```python
import math
import jax
import jax.numpy as jnp
from jax import lax

D_T = 4608
D_S = 3584
VOCAB_DEV = 512
TOKENS = 512
VOCAB = 16384
N_COL = 2


def build_table(key, width, model_tag):
    table_key = jax.random.fold_in(key, 11 + model_tag)
    slope = 0.6 + 1.2 * jnp.arange(VOCAB, dtype=jnp.float32) / VOCAB
    entries = jnp.clip(jax.random.normal(table_key, (VOCAB, width), jnp.float32), -6.0, 6.0)
    table = entries * slope[:, None] * (3.0 / math.sqrt(width))
    return table


def build_states(key, width, model_tag):
    state_key = jax.random.fold_in(key, 23 + model_tag)
    key_values = jax.random.fold_in(state_key, 0)
    states = jnp.clip(jax.random.normal(key_values, (TOKENS, width), jnp.float32), -6.0, 6.0)
    return states


def draw_teacher_hidden(key, part):
    return build_states(key, D_T, 0).astype(jnp.bfloat16)


def draw_student_hidden(key, part):
    return build_states(key, D_S, 1).astype(jnp.bfloat16)


def draw_teacher_embed(key, part):
    return build_table(key, D_T, 0).astype(jnp.bfloat16)


def draw_student_embed(key, part):
    return build_table(key, D_S, 1).astype(jnp.bfloat16)


def setup_inputs(seed: int = 0) -> dict:
    arg_keys = jax.random.split(jax.random.key(seed), 5)
    return {
        "teacher_hidden": draw_teacher_hidden(jax.random.fold_in(arg_keys[4], 71), 0),
        "student_hidden": draw_student_hidden(jax.random.fold_in(arg_keys[4], 71), 0),
        "teacher_embed": draw_teacher_embed(jax.random.fold_in(arg_keys[4], 71), 0),
        "student_embed": draw_student_embed(jax.random.fold_in(arg_keys[4], 71), 0),
    }


def reference(teacher_hidden, student_hidden, teacher_embed, student_embed):
    width_block = VOCAB_DEV * N_COL
    blocks = VOCAB // width_block
    teacher_blocks = teacher_embed.reshape(blocks, width_block, D_T)
    student_blocks = student_embed.reshape(blocks, width_block, D_S)

    def advance(running, tables):
        top_teacher, sum_teacher, cross_term, top_student, sum_student = running
        logit_teacher = jnp.dot(teacher_hidden, tables[0].T, preferred_element_type=jnp.float32)
        logit_student = jnp.dot(student_hidden, tables[1].T, preferred_element_type=jnp.float32)
        high_teacher = jnp.maximum(top_teacher, jnp.max(logit_teacher, 1))
        high_student = jnp.maximum(top_student, jnp.max(logit_student, 1))
        weights = jnp.exp(logit_teacher - high_teacher[:, None])
        decay_teacher = jnp.exp(top_teacher - high_teacher)
        decay_student = jnp.exp(top_student - high_student)
        sum_teacher = sum_teacher * decay_teacher + jnp.sum(weights, 1)
        cross_term = cross_term * decay_teacher + jnp.sum(weights * (logit_teacher - logit_student), 1)
        sum_student = sum_student * decay_student + jnp.sum(jnp.exp(logit_student - high_student[:, None]), 1)
        return (high_teacher, sum_teacher, cross_term, high_student, sum_student), None

    lowest = jnp.full((TOKENS,), -1e30, jnp.float32)
    nothing = jnp.zeros((TOKENS,), jnp.float32)
    finals, unused = lax.scan(advance, (lowest, nothing, nothing, lowest, nothing), (teacher_blocks, student_blocks))
    top_teacher, sum_teacher, cross_term, top_student, sum_student = finals
    divergence = cross_term / sum_teacher - top_teacher - jnp.log(sum_teacher) + top_student + jnp.log(sum_student)
    return divergence, jnp.mean(divergence)
```

```python
import functools
import jax
import jax.numpy as jnp
from jax import lax
from jax.experimental import pallas as pl
from jax.experimental.pallas import tpu as pltpu
from jax.sharding import PartitionSpec as P

MESH = pl.DeviceIdType.MESH
CORES = 2
SIDE = 2
WIDTH = 256
ORDERS = ("xzy", "zyx", "zxy", "yzx", "zxy", "zyx", "zxy", "zyx")
AHEAD = 6
LAGS = (0, 1, 3, 4)


def whole_stats(logit_teacher, logit_student):
    top_teacher = jnp.max(logit_teacher, 0, keepdims=True)
    top_student = jnp.max(logit_student, 0, keepdims=True)
    weights = jnp.exp(logit_teacher - top_teacher)
    sum_teacher = jnp.sum(weights, 0, keepdims=True)
    cross_term = jnp.sum(weights * (logit_teacher - logit_student), 0, keepdims=True)
    sum_student = jnp.sum(jnp.exp(logit_student - top_student), 0, keepdims=True)
    return top_teacher, sum_teacher, cross_term, top_student, sum_student


def merge(parts):
    tops_teacher = [part[0:1, :] for part in parts]
    tops_student = [part[3:4, :] for part in parts]
    top_teacher = functools.reduce(jnp.maximum, tops_teacher)
    top_student = functools.reduce(jnp.maximum, tops_student)
    scale_teacher = [jnp.exp(top - top_teacher) for top in tops_teacher]
    scale_student = [jnp.exp(top - top_student) for top in tops_student]
    sum_teacher = sum(part[1:2, :] * scale for part, scale in zip(parts, scale_teacher))
    cross_term = sum(part[2:3, :] * scale for part, scale in zip(parts, scale_teacher))
    sum_student = sum(part[4:5, :] * scale for part, scale in zip(parts, scale_student))
    return top_teacher, sum_teacher, cross_term, top_student, sum_student


def kernel(depth, n_col, teacher_hidden, student_hidden, teacher_embed, student_embed, out, states,
           teacher_table, student_table, logits, plane, line, own_sem, table_sem,
           send_sem, recv_sem, core_send, core_recv, stat_send, stat_recv):
    row, y = lax.axis_index("row"), lax.axis_index("col")
    z, x, c = row // (SIDE * CORES), (row // CORES) % SIDE, row % CORES
    sizes = {"z": depth, "x": SIDE, "y": n_col}
    here = {"z": z, "x": x, "y": y}
    n_teacher = teacher_hidden.shape[1] // WIDTH
    n_student = student_hidden.shape[1] // WIDTH
    chunks = n_teacher + n_student
    tokens = logits.shape[2]

    own_copies = []
    for k in range(chunks):
        source, first = (teacher_hidden, k) if k < n_teacher else (student_hidden, k - n_teacher)
        copy = pltpu.make_async_copy(
            source.at[:, pl.ds(first * WIDTH, WIDTH)], states.at[k, y, z, x, c], own_sem.at[k]
        )
        copy.start()
        own_copies.append(copy)
    tables = [
        pltpu.make_async_copy(teacher_embed, teacher_table, table_sem.at[0]),
        pltpu.make_async_copy(student_embed, student_table, table_sem.at[1]),
    ]
    for copy in tables:
        copy.start()

    def device(z=z, x=x, c=c, y=y):
        return ((z * SIDE + x) * CORES + c, y)

    group = SIDE * CORES * n_col
    spot = (x * CORES + c) * n_col + y

    def in_plane(place):
        place = lax.rem(place, group)
        return device(x=place // (CORES * n_col), c=(place // n_col) % CORES, y=place % n_col)

    def on_axis(axis, step):
        return {axis: lax.rem(here[axis] + step, sizes[axis])}

    barrier = pltpu.get_barrier_semaphore()
    for step in range(1, group):
        pl.semaphore_signal(barrier, inc=1, device_id=in_plane(spot + step), device_id_type=MESH)
    for step in range(1, depth):
        pl.semaphore_signal(
            barrier, inc=1, device_id=device(**on_axis("z", step)), device_id_type=MESH
        )
    pl.semaphore_wait(barrier, group + depth - 2)

    started = []

    def region(k, done, at):
        index = [slice(None) if axis in done else at[axis] for axis in "yzx"]
        return states.at[(k, *index, c)]

    def base(order, phase):
        return sum(sizes[axis] - 1 for axis in order[:phase])

    def send(k, phase):
        order = ORDERS[k % len(ORDERS)]
        axis, done = order[phase], order[:phase]
        for step in range(1, sizes[axis]):
            slot = base(order, phase) + step - 1
            block = region(k, done, here)
            copy = pltpu.make_async_remote_copy(
                src_ref=block, dst_ref=block, send_sem=send_sem.at[k, slot],
                recv_sem=recv_sem.at[k, slot], device_id=device(**on_axis(axis, step)),
                device_id_type=MESH,
            )
            copy.start()
            started.append(copy)

    def receive(k, phase):
        order = ORDERS[k % len(ORDERS)]
        axis, done = order[phase], order[:phase]
        for step in range(1, sizes[axis]):
            slot = base(order, phase) + step - 1
            source = dict(here)
            source[axis] = lax.rem(here[axis] - step + sizes[axis], sizes[axis])
            block = region(k, done, source)
            pltpu.make_async_remote_copy(
                src_ref=block, dst_ref=block, send_sem=send_sem.at[k, slot],
                recv_sem=recv_sem.at[k, slot], device_id=device(), device_id_type=MESH,
            ).wait_recv()

    def hand_over(k):
        block = states.at[k, :, :, :, c]
        copy = pltpu.make_async_remote_copy(
            src_ref=block, dst_ref=block, send_sem=core_send.at[k], recv_sem=core_recv.at[k],
            device_id=device(c=1 - c), device_id_type=MESH,
        )
        copy.start()
        started.append(copy)

    def take_over(k):
        block = states.at[k, :, :, :, 1 - c]
        pltpu.make_async_remote_copy(
            src_ref=block, dst_ref=block, send_sem=core_send.at[k], recv_sem=core_recv.at[k],
            device_id=device(), device_id_type=MESH,
        ).wait_recv()

    def multiply(k):
        model, first, table = (
            (0, k, teacher_table) if k < n_teacher else (1, k - n_teacher, student_table)
        )
        if first == 0:
            tables[model].wait()
        share = table.shape[1] // n_col
        weights = jnp.concatenate(
            [table[:, j * share + first * WIDTH : j * share + (first + 1) * WIDTH] for j in range(n_col)], 1
        )
        hidden = jnp.concatenate(
            [states[k, j].reshape(tokens, WIDTH) for j in range(n_col)], 1
        )
        product = lax.dot_general(
            weights, hidden, (((1,), (1,)), ((), ())), preferred_element_type=jnp.float32
        )
        if first == 0:
            logits[model] = product
        else:
            logits[model] += product

    for k in range(min(AHEAD, chunks)):
        own_copies[k].wait()
        send(k, 0)
    for tick in range(chunks + LAGS[3]):
        k = tick + AHEAD
        if k < chunks:
            own_copies[k].wait()
            send(k, 0)
        k = tick - LAGS[0]
        if 0 <= k < chunks:
            receive(k, 0)
            send(k, 1)
        k = tick - LAGS[1]
        if 0 <= k < chunks:
            receive(k, 1)
            send(k, 2)
        k = tick - LAGS[2]
        if 0 <= k < chunks:
            receive(k, 2)
            hand_over(k)
        k = tick - LAGS[3]
        if 0 <= k < chunks:
            take_over(k)
            multiply(k)

    def token_block(j, carry):
        columns = pl.ds(pl.multiple_of(j * 128, 128), 128)
        stats = whole_stats(logits[0, :, columns], logits[1, :, columns])
        for i, value in enumerate(stats):
            plane[spot, i : i + 1, columns] = value
        return carry

    lax.fori_loop(0, tokens // 128, token_block, 0)

    def exchange(buffer, mine, count, target, first):
        for step in range(1, count):
            copy = pltpu.make_async_remote_copy(
                src_ref=buffer.at[mine], dst_ref=buffer.at[mine],
                send_sem=stat_send.at[first + step], recv_sem=stat_recv.at[first + step],
                device_id=target(step), device_id_type=MESH,
            )
            copy.start()
            started.append(copy)
        for step in range(1, count):
            source = lax.rem(mine - step + count, count)
            pltpu.make_async_remote_copy(
                src_ref=buffer.at[source], dst_ref=buffer.at[source],
                send_sem=stat_send.at[first + step], recv_sem=stat_recv.at[first + step],
                device_id=device(), device_id_type=MESH,
            ).wait_recv()

    exchange(plane, spot, group, lambda step: in_plane(spot + step), 0)
    for i, value in enumerate(merge([plane.at[j] for j in range(group)])):
        line[z, i : i + 1, :] = value
    exchange(line, z, depth, lambda step: device(**on_axis("z", step)), group)
    top_teacher, sum_teacher, cross_term, top_student, sum_student = merge(
        [line.at[j] for j in range(depth)]
    )
    divergence = (
        cross_term / sum_teacher - top_teacher - jnp.log(sum_teacher)
        + top_student + jnp.log(sum_student)
    )
    out[0:1, :] = divergence
    out[1:2, :] = jnp.broadcast_to(jnp.mean(divergence, axis=1, keepdims=True), (1, tokens))
    for copy in started:
        copy.wait_send()


def fused(teacher_hidden, student_hidden, teacher_embed, student_embed):
    n_row, n_col = lax.axis_size("row"), lax.axis_size("col")
    depth = n_row // (SIDE * CORES)
    block = teacher_hidden.shape[0]
    tokens = block * n_row
    chunks = (teacher_hidden.shape[1] + student_hidden.shape[1]) // WIDTH
    vocab = teacher_embed.shape[0]
    group = SIDE * CORES * n_col
    hops = depth + SIDE + n_col - 3
    dma = pltpu.SemaphoreType.DMA
    out = pl.pallas_call(
        functools.partial(kernel, depth, n_col),
        out_shape=jax.ShapeDtypeStruct((2, tokens), jnp.float32),
        in_specs=[pl.BlockSpec(memory_space=pl.ANY)] * 4,
        out_specs=pl.BlockSpec(memory_space=pltpu.VMEM),
        scratch_shapes=[
            pltpu.VMEM((chunks, n_col, depth, SIDE, CORES, block, WIDTH), jnp.bfloat16),
            pltpu.VMEM(teacher_embed.shape, jnp.bfloat16),
            pltpu.VMEM(student_embed.shape, jnp.bfloat16),
            pltpu.VMEM((2, vocab, tokens), jnp.float32),
            pltpu.VMEM((group, 8, tokens), jnp.float32),
            pltpu.VMEM((depth, 8, tokens), jnp.float32),
            dma((chunks,)),
            dma((2,)),
            dma((chunks, hops)),
            dma((chunks, hops)),
            dma((chunks,)),
            dma((chunks,)),
            dma((group + depth,)),
            dma((group + depth,)),
        ],
        compiler_params=pltpu.CompilerParams(
            collective_id=0, has_side_effects=True, vmem_limit_bytes=60 * 2**20
        ),
    )(teacher_hidden, student_hidden, teacher_embed, student_embed)
    own_count = tokens // (n_row * n_col)
    own_block = lax.axis_index("row") * n_col + lax.axis_index("col")
    return lax.dynamic_slice_in_dim(out[0], own_block * own_count, own_count), out[1, 0]


def block_stats(logit_teacher, logit_student):
    return tuple(value[:, 0] for value in whole_stats_rows(logit_teacher, logit_student))


def whole_stats_rows(logit_teacher, logit_student):
    return tuple(value.T for value in whole_stats(logit_teacher.T, logit_student.T))


def gathered(teacher_hidden, student_hidden, teacher_embed, student_embed):
    tokens = teacher_hidden.shape[0] * lax.axis_size("row")
    logit_teacher, logit_student = (
        jnp.einsum(
            "td,vd->tv",
            lax.all_gather(lax.all_gather(hidden, "col", axis=1, tiled=True), "row", axis=0, tiled=True),
            embed,
            preferred_element_type=jnp.float32,
        )
        for hidden, embed in ((teacher_hidden, teacher_embed), (student_hidden, student_embed))
    )
    top_teacher, sum_teacher, cross_term, top_student, sum_student = block_stats(
        logit_teacher, logit_student
    )
    high_teacher, high_student = lax.pmax((top_teacher, top_student), ("row", "col"))
    teacher_scale = jnp.exp(top_teacher - high_teacher)
    student_scale = jnp.exp(top_student - high_student)
    sum_teacher, cross_term, sum_student = lax.psum(
        (sum_teacher * teacher_scale, cross_term * teacher_scale, sum_student * student_scale),
        ("row", "col"),
    )
    divergence = (
        cross_term / sum_teacher - high_teacher - jnp.log(sum_teacher)
        + high_student + jnp.log(sum_student)
    )
    own_count = tokens // (lax.axis_size("row") * lax.axis_size("col"))
    own_block = lax.axis_index("row") * lax.axis_size("col") + lax.axis_index("col")
    return (
        lax.dynamic_slice_in_dim(divergence, own_block * own_count, own_count),
        jnp.mean(divergence),
    )


def per_device(teacher_hidden, student_hidden, teacher_embed, student_embed):
    whole = all(hidden.shape[1] % WIDTH == 0 for hidden in (teacher_hidden, student_hidden))
    plan = fused if whole and lax.axis_size("row") % (SIDE * CORES) == 0 else gathered
    return plan(teacher_hidden, student_hidden, teacher_embed, student_embed)


def solution(mesh):
    return jax.shard_map(
        per_device,
        mesh=mesh,
        in_specs=(
            P("row", "col"),
            P("row", "col"),
            P(("row", "col"), None),
            P(("row", "col"), None),
        ),
        out_specs=(P(("row", "col")), P()),
        check_vma=False,
    )
```

```python
import functools
import jax
import jax.numpy as jnp
from jax import lax
from jax.experimental import pallas as pl
from jax.experimental.pallas import tpu as pltpu
from jax.sharding import PartitionSpec as P

MESH = pl.DeviceIdType.MESH
CORES = 2
SIDE = 2
WIDTH = 256
LATE = 2
AHEAD = 6
LAGS = (0, 2, 4, 5)
LANES = 128


def whole_stats(logit_teacher, logit_student):
    top_teacher = jnp.max(logit_teacher, 0, keepdims=True)
    top_student = jnp.max(logit_student, 0, keepdims=True)
    weights = jnp.exp(logit_teacher - top_teacher)
    sum_teacher = jnp.sum(weights, 0, keepdims=True)
    cross_term = jnp.sum(weights * (logit_teacher - logit_student), 0, keepdims=True)
    sum_student = jnp.sum(jnp.exp(logit_student - top_student), 0, keepdims=True)
    return top_teacher, sum_teacher, cross_term, top_student, sum_student


def merge_tops(parts, top_row, sum_row, blocks):
    tops = [part[top_row * blocks : (top_row + 1) * blocks, :] for part in parts]
    sums = [part[sum_row * blocks : (sum_row + 1) * blocks, :] for part in parts]
    top = functools.reduce(jnp.maximum, tops)
    return top, sum(value * jnp.exp(old - top) for value, old in zip(sums, tops))


def kernel(depth, n_col, teacher_hidden, student_hidden, teacher_embed, student_embed, out, out_mean,
           states, teacher_table, student_table, logits, weights, totals, plane_t, line_t, plane_s,
           line_s, own_sem, table_sem, send_sem, recv_sem, core_send, core_recv, stat_send, stat_recv):
    row, y = lax.axis_index("row"), lax.axis_index("col")
    z, x, c = row // (SIDE * CORES), (row // CORES) % SIDE, row % CORES
    sizes = {"z": depth, "x": SIDE, "y": n_col}
    here = {"z": z, "x": x, "y": y}
    n_teacher = teacher_hidden.shape[1] // WIDTH
    n_student = student_hidden.shape[1] // WIDTH
    chunks = n_teacher + n_student
    tokens = logits.shape[2]
    blocks = tokens // LANES

    own_copies = []
    for k in range(chunks):
        source, first = (teacher_hidden, k) if k < n_teacher else (student_hidden, k - n_teacher)
        own_copies.append(pltpu.make_async_copy(
            source.at[:, pl.ds(first * WIDTH, WIDTH)], states.at[k, y, z, x, c], own_sem.at[k]
        ))
    late = list(range(chunks - LATE, chunks))
    early = list(range(chunks - LATE))
    for k in late + early:
        own_copies[k].start()
    tables = [
        pltpu.make_async_copy(teacher_embed, teacher_table, table_sem.at[0]),
        pltpu.make_async_copy(student_embed, student_table, table_sem.at[1]),
    ]
    for copy in tables:
        copy.start()

    def device(z=z, x=x, c=c, y=y):
        return ((z * SIDE + x) * CORES + c, y)

    group = SIDE * CORES * n_col
    spot = (x * CORES + c) * n_col + y

    def in_plane(place):
        place = lax.rem(place, group)
        return device(x=place // (CORES * n_col), c=(place // n_col) % CORES, y=place % n_col)

    def shifted(axis, step):
        return lax.rem(here[axis] + step + sizes[axis], sizes[axis])

    barrier = pltpu.get_barrier_semaphore()
    for step in range(1, group):
        pl.semaphore_signal(barrier, inc=1, device_id=in_plane(spot + step), device_id_type=MESH)
    for step in range(1, depth):
        pl.semaphore_signal(
            barrier, inc=1, device_id=device(z=shifted("z", step)), device_id_type=MESH
        )
    pl.semaphore_wait(barrier, group + depth - 2)

    started = []
    everything = slice(None)

    def own(at):
        return at["y"], at["z"], at["x"]

    def z_line(at):
        return at["y"], everything, at["x"]

    def square(at):
        return everything, at["z"], everything

    def by_x(picked, *lanes):
        return lambda at: (at["y"], picked(at), 1 - at["x"], *lanes)

    def by_y(step, picked, *lanes):
        return lambda at: (lax.rem(at["y"] + n_col - step, n_col), picked(at), at["x"], *lanes)

    along_z = [("z", step) for step in range(1, depth)]
    across = [("x", 1)] + [("y", step) for step in range(1, n_col)]
    low = lambda at: slice(0, depth // 2)
    high = lambda at: slice(depth // 2, depth)
    same = lambda at: at["z"]
    rows_all = slice(None)
    left, right = (rows_all, slice(0, WIDTH // 2)), (rows_all, slice(WIDTH // 2, WIDTH))
    others = range(1, n_col)
    plan_early = (
        [(*hop, own) for hop in along_z],
        [(*hop, z_line) for hop in across],
        [("y", step, by_x(low)) for step in others] + [("x", 1, by_y(step, high)) for step in others],
    )
    plan_late = (
        [(*hop, own) for hop in across],
        [("y", step, by_x(same, *left)) for step in others]
        + [("x", 1, by_y(step, same, *right)) for step in others],
        [(*hop, square) for hop in along_z],
    )

    def transfers(k, phase):
        plan = plan_late if k in late else plan_early
        slot = sum(len(part) for part in plan[:phase])
        return [(slot + i, *entry) for i, entry in enumerate(plan[phase])]

    def remote(k, slot, index, target):
        block = states.at[(k, *index[:3], c, *index[3:])]
        return pltpu.make_async_remote_copy(
            src_ref=block, dst_ref=block, send_sem=send_sem.at[k, slot],
            recv_sem=recv_sem.at[k, slot], device_id=target, device_id_type=MESH,
        )

    def send(k, phase):
        if phase == 0:
            own_copies[k].wait()
        for slot, axis, step, index in transfers(k, phase):
            copy = remote(k, slot, index(here), device(**{axis: shifted(axis, step)}))
            copy.start()
            started.append(copy)

    def receive(k, phase):
        for slot, axis, step, index in transfers(k, phase):
            remote(k, slot, index({**here, axis: shifted(axis, -step)}), device()).wait_recv()

    def core_copy(k, of, target):
        block = states.at[k, :, :, :, of]
        return pltpu.make_async_remote_copy(
            src_ref=block, dst_ref=block, send_sem=core_send.at[k], recv_sem=core_recv.at[k],
            device_id=target, device_id_type=MESH,
        )

    def hand_over(k):
        copy = core_copy(k, c, device(c=1 - c))
        copy.start()
        started.append(copy)

    def multiply(k):
        core_copy(k, 1 - c, device()).wait_recv()
        model, first, table = (
            (0, k, teacher_table) if k < n_teacher else (1, k - n_teacher, student_table)
        )
        if first == 0:
            tables[model].wait()
        share = table.shape[1] // n_col
        columns = jnp.concatenate(
            [table[:, j * share + first * WIDTH : j * share + (first + 1) * WIDTH] for j in range(n_col)], 1
        )
        hidden = jnp.concatenate([states[k, j].reshape(tokens, WIDTH) for j in range(n_col)], 1)
        product = lax.dot_general(
            columns, hidden, (((1,), (1,)), ((), ())), preferred_element_type=jnp.float32
        )
        if first == 0:
            logits[model] = product
        else:
            logits[model] += product

    def stat_copy(buffer, place, sem, target):
        return pltpu.make_async_remote_copy(
            src_ref=buffer.at[place], dst_ref=buffer.at[place], send_sem=stat_send.at[sem],
            recv_sem=stat_recv.at[sem], device_id=target, device_id_type=MESH,
        )

    def give_stats(buffer, mine, count, target, base):
        for step in range(1, count):
            copy = stat_copy(buffer, mine, base + step, target(step))
            copy.start()
            started.append(copy)

    def take_stats(buffer, mine, count, base):
        for step in range(1, count):
            source = lax.rem(mine - step + count, count)
            stat_copy(buffer, source, base + step, device()).wait_recv()

    def to_plane(step):
        return in_plane(spot + step)

    def to_line(step):
        return device(z=shifted("z", step))

    def lanes_of(j):
        return pl.ds(pl.multiple_of(j * LANES, LANES), LANES)

    def teacher_local():
        def token_block(j, carry):
            values = logits[0, :, lanes_of(j)]
            top = jnp.max(values, 0, keepdims=True)
            plane_t[spot, pl.ds(j, 1), :] = top
            plane_t[spot, pl.ds(blocks + j, 1), :] = jnp.sum(jnp.exp(values - top), 0, keepdims=True)
            return carry

        lax.fori_loop(0, blocks, token_block, 0)
        give_stats(plane_t, spot, group, to_plane, 0)

    def teacher_plane():
        take_stats(plane_t, spot, group, 0)
        top, total = merge_tops([plane_t.at[j] for j in range(group)], 0, 1, blocks)
        line_t[z, 0:blocks, :] = top
        line_t[z, blocks : 2 * blocks, :] = total
        give_stats(line_t, z, depth, to_line, group)

    def teacher_line():
        take_stats(line_t, z, depth, group)
        top, total = merge_tops([line_t.at[j] for j in range(depth)], 0, 1, blocks)
        totals[0:blocks, :] = top
        totals[blocks : 2 * blocks, :] = total

        def token_block(j, carry):
            weights[:, lanes_of(j)] = jnp.exp(logits[0, :, lanes_of(j)] - totals[pl.ds(j, 1), :])
            return carry

        lax.fori_loop(0, blocks, token_block, 0)

    agenda = {n_teacher - 1: teacher_local, n_teacher + 1: teacher_plane, n_teacher + 3: teacher_line}

    def finish(k):
        multiply(k)
        if k in agenda:
            agenda[k]()

    for k in late:
        send(k, 0)
    for k in early[:AHEAD]:
        send(k, 0)
    for tick in range(len(early) + LAGS[3]):
        if 0 <= tick + AHEAD < len(early):
            send(early[tick + AHEAD], 0)
        if tick - LAGS[0] in early:
            receive(tick - LAGS[0], 0)
            send(tick - LAGS[0], 1)
        if tick - LAGS[1] in early:
            receive(tick - LAGS[1], 1)
            send(tick - LAGS[1], 2)
        if tick == 0:
            for k in late:
                receive(k, 0)
                send(k, 1)
        if tick == max(len(early) - AHEAD, 1):
            for k in late:
                receive(k, 1)
                send(k, 2)
        if tick - LAGS[2] in early:
            receive(tick - LAGS[2], 2)
            hand_over(tick - LAGS[2])
        if tick - LAGS[3] in early:
            finish(tick - LAGS[3])
    for k in late:
        receive(k, 2)
        hand_over(k)
    for k in late:
        finish(k)

    def token_block(j, carry):
        student = logits[1, :, lanes_of(j)]
        gap = logits[0, :, lanes_of(j)] - student
        top = jnp.max(student, 0, keepdims=True)
        plane_s[spot, pl.ds(j, 1), :] = top
        plane_s[spot, pl.ds(blocks + j, 1), :] = jnp.sum(jnp.exp(student - top), 0, keepdims=True)
        plane_s[spot, pl.ds(2 * blocks + j, 1), :] = jnp.sum(
            weights[:, lanes_of(j)] * gap, 0, keepdims=True
        )
        return carry

    lax.fori_loop(0, blocks, token_block, 0)

    def merge_student(parts):
        top, total = merge_tops(parts, 0, 1, blocks)
        return top, total, sum(part[2 * blocks : 3 * blocks, :] for part in parts)

    base = group + depth
    give_stats(plane_s, spot, group, to_plane, base)
    take_stats(plane_s, spot, group, base)
    for i, value in enumerate(merge_student([plane_s.at[j] for j in range(group)])):
        line_s[z, i * blocks : (i + 1) * blocks, :] = value
    give_stats(line_s, z, depth, to_line, base + group)
    take_stats(line_s, z, depth, base + group)
    top_student, sum_student, cross_term = merge_student([line_s.at[j] for j in range(depth)])
    top_teacher, sum_teacher = totals[0:blocks, :], totals[blocks : 2 * blocks, :]
    divergence = (
        cross_term / sum_teacher - top_teacher - jnp.log(sum_teacher)
        + top_student + jnp.log(sum_student)
    )
    out_mean[...] = jnp.sum(jnp.sum(divergence, 1, keepdims=True), 0, keepdims=True) / tokens
    count = out.shape[1]
    mine = row * n_col + y
    per_block = LANES // count
    own_row = lax.broadcasted_iota(jnp.int32, divergence.shape, 0) == mine // per_block
    own_line = jnp.sum(jnp.where(own_row, divergence, 0.0), 0, keepdims=True)
    result = own_line[:, 0:count]
    for i in range(1, per_block):
        here_it_is = lax.rem(mine, per_block) == i
        result = jnp.where(here_it_is, own_line[:, i * count : (i + 1) * count], result)
    out[...] = result
    for copy in started:
        copy.wait_send()


def fused(teacher_hidden, student_hidden, teacher_embed, student_embed):
    n_row, n_col = lax.axis_size("row"), lax.axis_size("col")
    depth = n_row // (SIDE * CORES)
    block = teacher_hidden.shape[0]
    tokens = block * n_row
    own_count = tokens // (n_row * n_col)
    chunks = (teacher_hidden.shape[1] + student_hidden.shape[1]) // WIDTH
    vocab = teacher_embed.shape[0]
    group = SIDE * CORES * n_col
    hops = depth + 3 * (n_col - 1)
    stats = 2 * (group + depth)
    blocks = tokens // LANES
    whole = -(-2 * blocks // 8) * 8
    tail = -(-3 * blocks // 8) * 8
    dma = pltpu.SemaphoreType.DMA
    divergence, mean_divergence = pl.pallas_call(
        functools.partial(kernel, depth, n_col),
        out_shape=(
            jax.ShapeDtypeStruct((1, own_count), jnp.float32),
            jax.ShapeDtypeStruct((1, 1), jnp.float32),
        ),
        in_specs=[pl.BlockSpec(memory_space=pl.ANY)] * 4,
        out_specs=(pl.BlockSpec(memory_space=pltpu.VMEM), pl.BlockSpec(memory_space=pltpu.VMEM)),
        scratch_shapes=[
            pltpu.VMEM((chunks, n_col, depth, SIDE, CORES, block, WIDTH), jnp.bfloat16),
            pltpu.VMEM(teacher_embed.shape, jnp.bfloat16),
            pltpu.VMEM(student_embed.shape, jnp.bfloat16),
            pltpu.VMEM((2, vocab, tokens), jnp.float32),
            pltpu.VMEM((vocab, tokens), jnp.float32),
            pltpu.VMEM((whole, LANES), jnp.float32),
            pltpu.VMEM((group, whole, LANES), jnp.float32),
            pltpu.VMEM((depth, whole, LANES), jnp.float32),
            pltpu.VMEM((group, tail, LANES), jnp.float32),
            pltpu.VMEM((depth, tail, LANES), jnp.float32),
            dma((chunks,)),
            dma((2,)),
            dma((chunks, hops)),
            dma((chunks, hops)),
            dma((chunks,)),
            dma((chunks,)),
            dma((stats,)),
            dma((stats,)),
        ],
        compiler_params=pltpu.CompilerParams(
            collective_id=0, has_side_effects=True, vmem_limit_bytes=60 * 2**20
        ),
    )(teacher_hidden, student_hidden, teacher_embed, student_embed)
    return divergence.reshape(own_count), mean_divergence.reshape(())


def block_stats(logit_teacher, logit_student):
    return tuple(value[:, 0] for value in whole_stats_rows(logit_teacher, logit_student))


def whole_stats_rows(logit_teacher, logit_student):
    return tuple(value.T for value in whole_stats(logit_teacher.T, logit_student.T))


def gathered(teacher_hidden, student_hidden, teacher_embed, student_embed):
    tokens = teacher_hidden.shape[0] * lax.axis_size("row")
    logit_teacher, logit_student = (
        jnp.einsum(
            "td,vd->tv",
            lax.all_gather(lax.all_gather(hidden, "col", axis=1, tiled=True), "row", axis=0, tiled=True),
            embed,
            preferred_element_type=jnp.float32,
        )
        for hidden, embed in ((teacher_hidden, teacher_embed), (student_hidden, student_embed))
    )
    top_teacher, sum_teacher, cross_term, top_student, sum_student = block_stats(
        logit_teacher, logit_student
    )
    high_teacher, high_student = lax.pmax((top_teacher, top_student), ("row", "col"))
    teacher_scale = jnp.exp(top_teacher - high_teacher)
    student_scale = jnp.exp(top_student - high_student)
    sum_teacher, cross_term, sum_student = lax.psum(
        (sum_teacher * teacher_scale, cross_term * teacher_scale, sum_student * student_scale),
        ("row", "col"),
    )
    divergence = (
        cross_term / sum_teacher - high_teacher - jnp.log(sum_teacher)
        + high_student + jnp.log(sum_student)
    )
    own_count = tokens // (lax.axis_size("row") * lax.axis_size("col"))
    own_block = lax.axis_index("row") * lax.axis_size("col") + lax.axis_index("col")
    return (
        lax.dynamic_slice_in_dim(divergence, own_block * own_count, own_count),
        jnp.mean(divergence),
    )


def per_device(teacher_hidden, student_hidden, teacher_embed, student_embed):
    n_row, n_col = lax.axis_size("row"), lax.axis_size("col")
    tokens = teacher_hidden.shape[0] * n_row
    own_count = tokens // (n_row * n_col)
    fits = (
        all(hidden.shape[1] % WIDTH == 0 for hidden in (teacher_hidden, student_hidden))
        and student_hidden.shape[1] // WIDTH >= LATE + 2
        and n_row % (2 * SIDE * CORES) == 0
        and n_col > 1
        and tokens % LANES == 0
        and LANES % own_count == 0
    )
    plan = fused if fits else gathered
    return plan(teacher_hidden, student_hidden, teacher_embed, student_embed)


def solution(mesh):
    return jax.shard_map(
        per_device,
        mesh=mesh,
        in_specs=(
            P("row", "col"),
            P("row", "col"),
            P(("row", "col"), None),
            P(("row", "col"), None),
        ),
        out_specs=(P(("row", "col")), P()),
        check_vma=False,
    )
```
